32 devices in a mesh: chan: 4 (over y, x), strip: 8 (over z, core).
Axes of the slice: x: 2, y: 2, z: 4, core: 2. Of those that a mesh axis runs over, the one named last changes fastest.
Arguments:
- wave_field: float32 [2, 16, 1536, 1536], P(None, 'chan', 'strip'), may hold values from -6 to 6
- radial_op: float32 [1536, 1536], replicated, may hold values from -1 to 1, as said below
- coupling: float32 [2, 16, 8], replicated, may hold values from -4 to 4
- couple: int32 [16, 8], replicated, may hold values from 0 to 15
- partner: int32 [16], replicated, may hold values from 0 to 15, as said below
- extent: int32 [16], replicated, may hold values from 384 to 1536, as said below
Outputs:
- first_step: float32 [2, 16, 1536, 1536], P(None, None, 'strip', 'chan')
- second_step: float32 [2, 16, 1536, 1536], P(None, None, 'strip', 'chan')
The draws below stay inside these ranges and needn't reach their ends.
Inputs may be any that keep to these rules, and one draw needn't show every extreme that they name: radial_op is symmetric. partner pairs the channels: partner(partner(c)) == c and partner(c) != c. Each extent is a multiple of 96; some channel has extent 1536 and some 1536 // 4.
All inputs are finite; a program needn't handle non-finite values.
Results may differ from the reference program's by a relative error of at most 0.0003.
Values sent between devices are 32-bit elements; how exact they have to be, the bound alone decides.
A program may use at most 256 MiB of HBM per device.

```python
import jax
import jax.numpy as jnp
from jax import lax

NR = 1536
CH = 16
MULT = 8


def draw_radial_op(key, part):
    noise = jnp.clip(jax.random.normal(key, (NR, NR), jnp.float32), -6.0, 6.0)
    sym = (noise + noise.T) * (0.35 / jnp.sqrt(2.0 * NR))
    diagonal = jax.random.uniform(jax.random.fold_in(key, 1), (NR,), jnp.float32, -0.5, 0.5)
    return sym + jnp.diag(diagonal)


def draw_partner(key, part):
    order = jax.random.permutation(key, CH).astype(jnp.int32)
    paired = jnp.zeros((CH,), jnp.int32)
    paired = paired.at[order[0::2]].set(order[1::2])
    paired = paired.at[order[1::2]].set(order[0::2])
    return paired


def draw_extent(key, part):
    steps = jax.random.randint(key, (CH,), 0, 13).astype(jnp.int32)
    order = jax.random.permutation(jax.random.fold_in(key, 1), CH).astype(jnp.int32)
    steps = steps.at[order[0]].set(0)
    steps = steps.at[order[1]].set(12)
    return (NR - steps * (NR // 16)).astype(jnp.int32)


def with_ends(array, key, least, largest):
    longest = array.shape.index(max(array.shape))
    spots = []
    for shift in (0, 1):
        where = [jax.random.randint(jax.random.fold_in(key, axis), (), 0, length) for axis, length in enumerate(array.shape)]
        where[longest] = (where[longest] + shift) % array.shape[longest]
        spots.append(tuple(where))
    return array.at[spots[0]].set(least).at[spots[1]].set(largest)


def block_scale(stream_key, shape, pieces, smallest, largest):
    def one(axis_at, blocks):
        steps = jax.random.uniform(jax.random.fold_in(jax.random.fold_in(stream_key, 6), axis_at), (blocks,), jnp.float32, smallest / len(pieces), largest / len(pieces))
        return jnp.repeat(jnp.exp(steps), shape[axis_at] // blocks).reshape((-1,) + (1,) * (len(shape) - axis_at - 1))

    factor_of = one(*pieces[0])
    for cut in pieces[1:]:
        factor_of = factor_of * one(*cut)
    return factor_of


def centred(key, dims, spread, most, cuts=(), dtype=jnp.bfloat16):
    values = jax.random.normal(key, dims, jnp.float32) * spread
    if len(cuts) > 0:
        values = block_scale(key, dims, cuts, -0.22, 0.18) * values
    return jnp.clip(values, min=-most, max=most).astype(dtype)


def setup_inputs(seed: int = 0) -> dict:
    arg_keys = jax.random.split(jax.random.key(seed), 7)
    return {
        "wave_field": centred(arg_keys[0], (2, CH, NR, NR), 1.0, 6.0, ((1, 4), (2, 8)), jnp.float32),
        "radial_op": draw_radial_op(jax.random.fold_in(arg_keys[6], 71), 0),
        "coupling": centred(arg_keys[2], (2, CH, MULT), 0.3, 4.0, (), jnp.float32),
        "couple": with_ends(jax.random.randint(arg_keys[3], (CH, MULT), 0, CH), jax.random.fold_in(arg_keys[3], 1), 0, CH - 1).astype(jnp.int32),
        "partner": draw_partner(jax.random.fold_in(arg_keys[6], 71), 0),
        "extent": draw_extent(jax.random.fold_in(arg_keys[6], 71), 0),
    }


def potentials(row_pos, col_pos, count, orders):
    spacing = 8.0 / count
    first = row_pos.astype(jnp.float32) * spacing
    second = col_pos.astype(jnp.float32) * spacing
    lesser = jnp.minimum(first[:, None], second[None, :])
    greater = jnp.maximum(first[:, None], second[None, :])
    root = jnp.sqrt(greater * greater + 1.0)
    result = []
    for order in range(orders):
        result.append(lesser ** order / root ** (order + 1))
    return result

def reference(wave_field, radial_op, coupling, couple, partner, extent):
    positions = jnp.arange(NR).astype(jnp.int32)
    pots = potentials(positions, positions, NR, MULT)

    def apply(field):
        image = jnp.einsum('ak,pckb->pcab', radial_op, field, precision=lax.Precision.HIGHEST)

        def single(channel):
            total = image[:, channel] + jnp.swapaxes(image[:, partner[channel]], 1, 2)
            real_part = total[0]
            imag_part = total[1]
            for order in range(MULT):
                source = field[:, couple[channel, order]]
                c_real = coupling[0, channel, order]
                c_imag = coupling[1, channel, order]
                real_part = real_part + pots[order] * (c_real * source[0] - c_imag * source[1])
                imag_part = imag_part + pots[order] * (c_real * source[1] + c_imag * source[0])
            live = (positions[:, None] < extent[channel]) & (positions[None, :] < extent[channel])
            return jnp.where(live[None], jnp.stack([real_part, imag_part]), 0.0)
        return jnp.moveaxis(lax.map(single, jnp.arange(CH).astype(jnp.int32)), 0, 1)
    first_step = apply(wave_field)
    second_step = 2.0 * apply(first_step) - wave_field
    return (first_step, second_step)
```

```python
import functools

import jax
import jax.numpy as jnp
from jax import lax
from jax.experimental import pallas as pl
from jax.experimental.pallas import tpu as pltpu
from jax.sharding import PartitionSpec as P


def potentials(row_pos, col_pos, count, orders):
    spacing = 8.0 / count
    first = row_pos.astype(jnp.float32) * spacing
    second = col_pos.astype(jnp.float32) * spacing
    lesser = jnp.minimum(first[:, None], second[None, :])
    greater = jnp.maximum(first[:, None], second[None, :])
    root = jnp.sqrt(greater * greater + 1.0)
    result = []
    for order in range(orders):
        result.append(lesser**order / root ** (order + 1))
    return result


def couple_terms(field, image_rows, mirrored, coupling, couple, partner, pots, live):
    total = image_rows + jnp.take(mirrored, partner, axis=1)
    real_part = total[0]
    imag_part = total[1]
    for order in range(len(pots)):
        source = jnp.take(field, couple[:, order], axis=1)
        c_real = coupling[0, :, order][:, None, None]
        c_imag = coupling[1, :, order][:, None, None]
        real_part = real_part + pots[order] * (c_real * source[0] - c_imag * source[1])
        imag_part = imag_part + pots[order] * (c_real * source[1] + c_imag * source[0])
    return jnp.where(live[None], jnp.stack([real_part, imag_part]), 0.0)


def radial_product(radial_op, block):
    return jnp.einsum("ak,pckb->pcab", radial_op, block, precision=lax.Precision.HIGHEST)


def spread_columns(field):
    strips = lax.axis_size("strip")
    local_chans = field.shape[1]
    local_rows = field.shape[2]
    grid = field.shape[3]
    piece = grid // (strips * strips)
    shaped = field.reshape(2, local_chans, local_rows, strips, strips, piece)
    return jnp.transpose(shaped, (0, 1, 2, 4, 3, 5)).reshape(2, local_chans, local_rows, grid)


def spread_tiles(image):
    chans = lax.axis_size("chan")
    strips = lax.axis_size("strip")
    local_chans = image.shape[1]
    grid = image.shape[2]
    width = image.shape[3]
    piece = grid // (strips * strips)
    ratio = strips // chans
    block = grid // chans
    direct_send = image.reshape(2, local_chans, strips, width, chans, ratio * piece)
    direct_send = jnp.transpose(direct_send, (0, 1, 4, 2, 3, 5)).reshape(
        2, local_chans, chans * strips, width, ratio * piece
    )
    mirror_send = image.reshape(2, local_chans, chans, block, strips, piece)
    mirror_send = jnp.transpose(mirror_send, (0, 1, 2, 4, 3, 5)).reshape(
        2, local_chans, chans * strips, block, piece
    )
    direct_got, mirror_got = (
        lax.all_to_all(direct_send, ("chan", "strip"), split_axis=2, concat_axis=2, tiled=True),
        lax.all_to_all(mirror_send, ("chan", "strip"), split_axis=2, concat_axis=2, tiled=True),
    )
    direct_got = direct_got.reshape(2, local_chans, chans, strips, width, ratio, piece)
    direct_tiles = jnp.transpose(direct_got, (0, 2, 1, 4, 5, 3, 6)).reshape(
        2, chans * local_chans, width, block
    )
    mirror_got = mirror_got.reshape(2, local_chans, chans, strips, block, piece)
    mirror_tiles = jnp.transpose(mirror_got, (0, 2, 1, 3, 5, 4)).reshape(
        2, chans * local_chans, width, block
    )
    return (direct_tiles, mirror_tiles)


def general(wave_field, radial_op, coupling, couple, partner, extent):
    chans = lax.axis_size("chan")
    grid = wave_field.shape[3]
    strip_rows = wave_field.shape[2]
    chan_cols = grid // chans
    row_pos = lax.axis_index("strip") * strip_rows + jnp.arange(strip_rows)
    col_pos = lax.axis_index("chan") * chan_cols + jnp.arange(chan_cols)
    pots = potentials(row_pos, col_pos, grid, coupling.shape[2])
    live = (row_pos[None, :, None] < extent[:, None, None]) & (
        col_pos[None, None, :] < extent[:, None, None]
    )

    def radial(block):
        return radial_product(radial_op, block)

    def product_columns(field_rows):
        return radial(lax.all_to_all(field_rows, "strip", split_axis=3, concat_axis=2, tiled=True))

    field_tiles = lax.all_to_all(wave_field, "chan", split_axis=3, concat_axis=1, tiled=True)
    rows_tiles, mirror_tiles = spread_tiles(product_columns(spread_columns(wave_field)))
    first_step = couple_terms(
        field_tiles, rows_tiles, mirror_tiles, coupling, couple, partner, pots, live
    )
    image = product_columns(
        spread_columns(lax.all_to_all(first_step, "chan", split_axis=1, concat_axis=3, tiled=True))
    )
    rows_tiles, mirror_tiles = spread_tiles(image)
    applied = couple_terms(
        first_step, rows_tiles, mirror_tiles, coupling, couple, partner, pots, live
    )
    second_step = 2.0 * applied - field_tiles
    return (first_step, second_step)


MESH = pl.DeviceIdType.MESH
ANY = pl.BlockSpec(memory_space=pl.ANY)


def rem(value, count):
    return lax.rem(value, count)


def greet(others):
    barrier = pltpu.get_barrier_semaphore()
    for other in others:
        pl.semaphore_signal(barrier, inc=1, device_id=other, device_id_type=MESH)
    pl.semaphore_wait(barrier, len(others))


def remote(source, target, send, recv, device):
    return pltpu.make_async_remote_copy(
        src_ref=source,
        dst_ref=target,
        send_sem=send,
        recv_sem=recv,
        device_id=device,
        device_id_type=MESH,
    )


def columns(block, width):
    return pl.ds(pl.multiple_of(block * width, 128), width)


def lines(block, height):
    return pl.ds(pl.multiple_of(block * height, 8), height)


def gather_kernel(chans, strips, x, y, f, zs, zr, cs, cr, ls):
    c = lax.axis_index("chan")
    s = lax.axis_index("strip")
    per = y.shape[0]
    width = y.shape[2]
    rows = x.shape[1]
    ring = [(c, rem(s + d, strips)) for d in range(1, strips)]
    plane = [(rem(c + r, chans), s) for r in range(1, chans)]
    greet(ring + plane)
    copies = []
    for d in range(1, strips):
        t = ring[d - 1][1]
        copies.append(
            remote(
                x.at[pl.ds(rem(t, 2) * per, per), :, columns(t // 2, width)],
                y.at[:, lines(s, rows), :],
                zs.at[d],
                zr.at[d],
                ring[d - 1],
            )
        )
    for r in range(1, chans):
        j = plane[r - 1][0]
        for p in range(2):
            copies.append(
                remote(
                    x.at[pl.ds(p * per, per), :, columns(j, width)],
                    f.at[p * chans + c],
                    cs.at[r * 2 + p],
                    cr.at[r * 2 + p],
                    plane[r - 1],
                )
            )
    copies.append(
        pltpu.make_async_copy(
            x.at[pl.ds(rem(s, 2) * per, per), :, columns(s // 2, width)],
            y.at[:, lines(s, rows), :],
            ls.at[0],
        )
    )
    for p in range(2):
        copies.append(
            pltpu.make_async_copy(
                x.at[pl.ds(p * per, per), :, columns(c, width)], f.at[p * chans + c], ls.at[1 + p]
            )
        )
    for copy in copies:
        copy.start()
    for copy in copies:
        copy.wait()


def image_kernel(chans, strips, i, it, w, mt, dd, zs, zr, ms, mr, fs, fr, ls):
    c = lax.axis_index("chan")
    s = lax.axis_index("strip")
    rows = w.shape[2]
    width = w.shape[3]
    group = s // 2
    member = rem(s, 2)
    ring = [(c, rem(s + d, strips)) for d in range(1, strips)]
    plane = [
        (rem(c + r, chans), group * 2 + rem(member + e, 2))
        for r in range(chans)
        for e in range(2)
    ]
    greet(ring + plane[2:])
    slot = member * chans + c
    hops = []
    for d in range(1, strips):
        t = ring[d - 1][1]
        hops.append(
            remote(i.at[:, lines(t, rows), :], w.at[s], zs.at[d], zr.at[d], ring[d - 1])
        )

    def mirror(k):
        j = plane[k][0]
        m = rem(member + k % 2, 2)
        part = it.at[:, lines(m, rows), columns(j, width)]
        if k == 0:
            return pltpu.make_async_copy(part, mt.at[slot], ls.at[2])
        return remote(part, mt.at[slot], ms.at[k], mr.at[k], plane[k])

    mirrors = [mirror(k) for k in range(2 * chans)]
    for hop in hops:
        hop.start()

    def forward(source, u):
        j = u // 2
        p = rem(u, 2)
        away = rem(j - c + chans, chans)

        @pl.when(away == 0)
        def _():
            pltpu.make_async_copy(source, dd.at[p * chans + c], ls.at[p]).start()

        @pl.when(away != 0)
        def _():
            k = away * 2 + p
            remote(source, dd.at[p * chans + c], fs.at[k], fr.at[k], (j, s)).start()

    forward(i.at[:, lines(s, rows), :], s)
    for copy in mirrors:
        copy.start()
    for d in range(1, strips):
        hops[d - 1].wait_recv()
        u = rem(s - d + strips, strips)
        forward(w.at[u], u)
    for hop in hops:
        hop.wait_send()
    for copy in mirrors:
        copy.wait()
    for p in range(2):
        pltpu.make_async_copy(w.at[0], dd.at[p * chans + c], ls.at[p]).wait()
        for r in range(1, chans):
            k = r * 2 + p
            from_chan = rem(c - r + chans, chans)
            remote(
                w.at[0], dd.at[p * chans + from_chan], fs.at[k], fr.at[k], (rem(c + r, chans), s)
            ).wait()


def back_kernel(chans, strips, v, w, y, cs, cr, zs, zr, ls):
    c = lax.axis_index("chan")
    s = lax.axis_index("strip")
    rows = v.shape[2]
    ring = [(c, rem(s + d, strips)) for d in range(1, strips)]
    plane = [(rem(c + r, chans), s) for r in range(1, chans)]
    greet(ring + plane)
    hops = {}
    for r in range(1, chans):
        j = plane[r - 1][0]
        for p in range(2):
            k = r * 2 + p
            hops[k] = remote(
                v.at[p * chans + j], w.at[p * chans + c], cs.at[k], cr.at[k], plane[r - 1]
            )
            hops[k].start()

    def forward(source, j, p):
        t = j * 2 + p
        away = rem(t - s + strips, strips)

        @pl.when(away == 0)
        def _():
            pltpu.make_async_copy(source, y.at[:, lines(s, rows), :], ls).start()

        @pl.when(away != 0)
        def _():
            remote(
                source, y.at[:, lines(s, rows), :], zs.at[away], zr.at[away], (c, t)
            ).start()

    for p in range(2):
        forward(v.at[p * chans + c], c, p)
    for r in range(1, chans):
        j = rem(c - r + chans, chans)
        for p in range(2):
            hops[r * 2 + p].wait_recv()
            forward(w.at[p * chans + j], j, p)
    for k in hops:
        hops[k].wait_send()
    pltpu.make_async_copy(v.at[0], y.at[:, lines(s, rows), :], ls).wait()
    for d in range(1, strips):
        u = rem(s - d + strips, strips)
        remote(
            v.at[0], y.at[:, lines(u, rows), :], zs.at[d], zr.at[d], (c, rem(s + d, strips))
        ).wait()


def exchange(kernel, ident, outs, sems, *operands):
    chans = lax.axis_size("chan")
    strips = lax.axis_size("strip")
    return pl.pallas_call(
        functools.partial(kernel, chans, strips),
        out_shape=[jax.ShapeDtypeStruct(shape, jnp.float32) for shape in outs],
        in_specs=[ANY] * len(operands),
        out_specs=[ANY] * len(outs),
        scratch_shapes=[pltpu.SemaphoreType.DMA(n) for n in sems],
        compiler_params=pltpu.CompilerParams(collective_id=ident, has_side_effects=True),
    )(*operands)


def couple_kernel(count, last, ints, reals, *refs):
    if last:
        field, direct, mirror, base, out, pots = refs
    else:
        field, direct, mirror, out, pots = refs
    channels, height, width = field.shape[1:]
    orders = pots.shape[0]
    spacing = 8.0 / count
    row = ints[0] + pl.program_id(0) * height
    row = row + lax.broadcasted_iota(jnp.int32, (height, width), 0)
    col = ints[1] + lax.broadcasted_iota(jnp.int32, (height, width), 1)
    first = row.astype(jnp.float32) * spacing
    second = col.astype(jnp.float32) * spacing
    greater = jnp.maximum(first, second)
    root = jnp.sqrt(greater * greater + 1.0)
    ratio = jnp.minimum(first, second) / root
    pot = 1.0 / root
    for order in range(orders):
        pots[order] = pot
        pot = pot * ratio
    reach = jnp.maximum(row, col)

    def channel(c, carry):
        other = ints[2 + c]
        real_part = direct[0, c] + mirror[0, other]
        imag_part = direct[1, c] + mirror[1, other]
        for order in range(orders):
            k = ints[2 + 2 * channels + c * orders + order]
            c_real = reals[c * orders + order]
            c_imag = reals[channels * orders + c * orders + order]
            pot = pots[order]
            s_real = pot * field[0, k]
            s_imag = pot * field[1, k]
            real_part = real_part + (c_real * s_real - c_imag * s_imag)
            imag_part = imag_part + (c_real * s_imag + c_imag * s_real)
        live = reach < ints[2 + channels + c]
        real_part = jnp.where(live, real_part, 0.0)
        imag_part = jnp.where(live, imag_part, 0.0)
        if last:
            real_part = 2.0 * real_part - base[0, c]
            imag_part = 2.0 * imag_part - base[1, c]
        out[0, c] = real_part
        out[1, c] = imag_part
        return carry

    lax.fori_loop(0, channels, channel, 0)


def couple_tiles(count, ints, reals, orders, arrays):
    last = len(arrays) == 4
    shape = arrays[0].shape
    height = 16
    block = pl.BlockSpec((2, shape[1], height, shape[3]), lambda n: (0, 0, n, 0))
    smem = pl.BlockSpec(memory_space=pltpu.SMEM)
    return pl.pallas_call(
        functools.partial(couple_kernel, count, last),
        grid=(shape[2] // height,),
        out_shape=jax.ShapeDtypeStruct(shape, jnp.float32),
        in_specs=[smem, smem] + [block] * len(arrays),
        out_specs=block,
        scratch_shapes=[pltpu.VMEM((orders, height, shape[3]), jnp.float32)],
    )(ints, reals, *arrays)


def radial_images(radial_op, block):
    image = jnp.einsum("ak,mkb->mab", radial_op, block, precision=lax.Precision.HIGH)
    return image, jnp.swapaxes(image, 1, 2)


def local(wave_field, radial_op, coupling, couple, partner, extent):
    chans = lax.axis_size("chan")
    strips = lax.axis_size("strip")
    per, rows, grid = wave_field.shape[1:]
    width = grid // chans
    orders = coupling.shape[2]
    tiles = (2 * chans, per, rows, width)
    whole = (2, chans * per, rows, width)
    tall = (per, grid, width)
    starts = jnp.stack([lax.axis_index("strip") * rows, lax.axis_index("chan") * width])
    ints = jnp.concatenate([starts.astype(jnp.int32), partner, extent, couple.reshape(-1)])
    reals = coupling.reshape(-1)

    def images(ident, block):
        image, turned = radial_images(radial_op, block)
        _, mirror, direct = exchange(
            image_kernel,
            ident,
            [(strips, per, rows, width), tiles, tiles],
            [(strips,), (strips,), (2 * chans,), (2 * chans,), (2 * chans,), (2 * chans,), (3,)],
            image,
            turned,
        )
        return direct.reshape(whole), mirror.reshape(whole)

    block, field = exchange(
        gather_kernel,
        0,
        [tall, tiles],
        [(strips,), (strips,), (2 * chans,), (2 * chans,), (3,)],
        wave_field.reshape(2 * per, rows, grid),
    )
    field = field.reshape(whole)
    direct, mirror = images(1, block)
    first_step = couple_tiles(grid, ints, reals, orders, (field, direct, mirror))
    _, block = exchange(
        back_kernel,
        2,
        [tiles, tall],
        [(2 * chans,), (2 * chans,), (strips,), (strips,), ()],
        first_step.reshape(tiles),
    )
    direct, mirror = images(1, block)
    second_step = couple_tiles(grid, ints, reals, orders, (first_step, direct, mirror, field))
    return (first_step, second_step)


def dispatch(wave_field, *rest):
    chans = lax.axis_size("chan")
    strips = lax.axis_size("strip")
    width = wave_field.shape[3] // chans
    if strips == 2 * chans and width % 128 == 0 and wave_field.shape[2] % 16 == 0:
        return local(wave_field, *rest)
    return general(wave_field, *rest)


def solution(mesh):
    placed = (P(None, "chan", "strip", None), P(), P(), P(), P(), P())
    return jax.shard_map(
        dispatch,
        mesh=mesh,
        in_specs=placed,
        out_specs=(P(None, None, "strip", "chan"), P(None, None, "strip", "chan")),
        check_vma=False,
    )
```

```python
import functools

import jax
import jax.numpy as jnp
from jax import lax
from jax.experimental import pallas as pl
from jax.experimental.pallas import tpu as pltpu
from jax.sharding import PartitionSpec as P


def potentials(row_pos, col_pos, count, orders):
    spacing = 8.0 / count
    first = row_pos.astype(jnp.float32) * spacing
    second = col_pos.astype(jnp.float32) * spacing
    lesser = jnp.minimum(first[:, None], second[None, :])
    greater = jnp.maximum(first[:, None], second[None, :])
    root = jnp.sqrt(greater * greater + 1.0)
    result = []
    for order in range(orders):
        result.append(lesser**order / root ** (order + 1))
    return result


def couple_terms(field, image_rows, mirrored, coupling, couple, partner, pots, live):
    total = image_rows + jnp.take(mirrored, partner, axis=1)
    real_part = total[0]
    imag_part = total[1]
    for order in range(len(pots)):
        source = jnp.take(field, couple[:, order], axis=1)
        c_real = coupling[0, :, order][:, None, None]
        c_imag = coupling[1, :, order][:, None, None]
        real_part = real_part + pots[order] * (c_real * source[0] - c_imag * source[1])
        imag_part = imag_part + pots[order] * (c_real * source[1] + c_imag * source[0])
    return jnp.where(live[None], jnp.stack([real_part, imag_part]), 0.0)


def radial_product(radial_op, block):
    return jnp.einsum("ak,pckb->pcab", radial_op, block, precision=lax.Precision.HIGHEST)


def spread_columns(field):
    strips = lax.axis_size("strip")
    local_chans = field.shape[1]
    local_rows = field.shape[2]
    grid = field.shape[3]
    piece = grid // (strips * strips)
    shaped = field.reshape(2, local_chans, local_rows, strips, strips, piece)
    return jnp.transpose(shaped, (0, 1, 2, 4, 3, 5)).reshape(2, local_chans, local_rows, grid)


def spread_tiles(image):
    chans = lax.axis_size("chan")
    strips = lax.axis_size("strip")
    local_chans = image.shape[1]
    grid = image.shape[2]
    width = image.shape[3]
    piece = grid // (strips * strips)
    ratio = strips // chans
    block = grid // chans
    direct_send = image.reshape(2, local_chans, strips, width, chans, ratio * piece)
    direct_send = jnp.transpose(direct_send, (0, 1, 4, 2, 3, 5)).reshape(
        2, local_chans, chans * strips, width, ratio * piece
    )
    mirror_send = image.reshape(2, local_chans, chans, block, strips, piece)
    mirror_send = jnp.transpose(mirror_send, (0, 1, 2, 4, 3, 5)).reshape(
        2, local_chans, chans * strips, block, piece
    )
    direct_got, mirror_got = (
        lax.all_to_all(direct_send, ("chan", "strip"), split_axis=2, concat_axis=2, tiled=True),
        lax.all_to_all(mirror_send, ("chan", "strip"), split_axis=2, concat_axis=2, tiled=True),
    )
    direct_got = direct_got.reshape(2, local_chans, chans, strips, width, ratio, piece)
    direct_tiles = jnp.transpose(direct_got, (0, 2, 1, 4, 5, 3, 6)).reshape(
        2, chans * local_chans, width, block
    )
    mirror_got = mirror_got.reshape(2, local_chans, chans, strips, block, piece)
    mirror_tiles = jnp.transpose(mirror_got, (0, 2, 1, 3, 5, 4)).reshape(
        2, chans * local_chans, width, block
    )
    return (direct_tiles, mirror_tiles)


def general(wave_field, radial_op, coupling, couple, partner, extent):
    chans = lax.axis_size("chan")
    grid = wave_field.shape[3]
    strip_rows = wave_field.shape[2]
    chan_cols = grid // chans
    row_pos = lax.axis_index("strip") * strip_rows + jnp.arange(strip_rows)
    col_pos = lax.axis_index("chan") * chan_cols + jnp.arange(chan_cols)
    pots = potentials(row_pos, col_pos, grid, coupling.shape[2])
    live = (row_pos[None, :, None] < extent[:, None, None]) & (
        col_pos[None, None, :] < extent[:, None, None]
    )

    def radial(block):
        return radial_product(radial_op, block)

    def product_columns(field_rows):
        return radial(lax.all_to_all(field_rows, "strip", split_axis=3, concat_axis=2, tiled=True))

    field_tiles = lax.all_to_all(wave_field, "chan", split_axis=3, concat_axis=1, tiled=True)
    rows_tiles, mirror_tiles = spread_tiles(product_columns(spread_columns(wave_field)))
    first_step = couple_terms(
        field_tiles, rows_tiles, mirror_tiles, coupling, couple, partner, pots, live
    )
    image = product_columns(
        spread_columns(lax.all_to_all(first_step, "chan", split_axis=1, concat_axis=3, tiled=True))
    )
    rows_tiles, mirror_tiles = spread_tiles(image)
    applied = couple_terms(
        first_step, rows_tiles, mirror_tiles, coupling, couple, partner, pots, live
    )
    second_step = 2.0 * applied - field_tiles
    return (first_step, second_step)


MESH = pl.DeviceIdType.MESH
ANY = pl.BlockSpec(memory_space=pl.ANY)


def rem(value, count):
    return lax.rem(value, count)


def greet(others):
    barrier = pltpu.get_barrier_semaphore()
    for other in others:
        pl.semaphore_signal(barrier, inc=1, device_id=other, device_id_type=MESH)
    pl.semaphore_wait(barrier, len(others))


def remote(source, target, send, recv, device):
    return pltpu.make_async_remote_copy(
        src_ref=source,
        dst_ref=target,
        send_sem=send,
        recv_sem=recv,
        device_id=device,
        device_id_type=MESH,
    )


def columns(block, width):
    return pl.ds(pl.multiple_of(block * width, 128), width)


def lines(block, height):
    return pl.ds(pl.multiple_of(block * height, 8), height)


def apply_kernel(first, chans, strips, *refs):
    v, r, extra, y, i, it, w, mt, dd = refs[:9]
    rf, rhi, rlo, vf, vhi, vlo, ibuf, tbuf = refs[9:17]
    cs, cr, zs, zr, hs, hr, ms, mr, fs, fr, lz, lc, lm, lf, lv = refs[17:]
    c = lax.axis_index("chan")
    s = lax.axis_index("strip")
    per, grid, width = y.shape
    rows = w.shape[2]
    group = s // 2
    member = rem(s, 2)
    slot = member * chans + c
    greet(
        [(c, rem(s + d, strips)) for d in range(1, strips)]
        + [(rem(c + k, chans), s) for k in range(1, chans)]
        + [(rem(c + k, chans), group * 2 + rem(member + 1, 2)) for k in range(1, chans)]
    )

    def across(ch, k, p):
        j = rem(c + k, chans)
        if first:
            source = v.at[p * per + ch, :, columns(j, width)]
        else:
            source = v.at[p * chans + j, ch]
        target = extra.at[p * chans + c, ch]
        if k == 0:
            return pltpu.make_async_copy(source, target, lc.at[ch, p])
        n = k * 2 + p
        return remote(source, target, cs.at[ch, n], cr.at[ch, n], (j, s))

    def along(ch, d):
        t = rem(s + d, strips)
        if first:
            source = v.at[rem(t, 2) * per + ch, :, columns(t // 2, width)]
        else:
            source = v.at[rem(t, 2) * chans + t // 2, ch]
        target = y.at[ch, lines(s, rows), :]
        if d == 0:
            return pltpu.make_async_copy(source, target, lz.at[ch])
        return remote(source, target, zs.at[ch, d], zr.at[ch, d], (c, t))

    def relay(source, ch, t):
        away = rem(t - s + strips, strips)
        target = y.at[ch, lines(s, rows), :]

        @pl.when(away == 0)
        def _():
            pltpu.make_async_copy(source, target, lz.at[ch]).start()

        @pl.when(away != 0)
        def _():
            remote(source, target, zs.at[ch, away], zr.at[ch, away], (c, t)).start()

    def back(ch, d):
        t = rem(s + d, strips)
        source = i.at[ch, lines(t, rows), :]
        return remote(source, w.at[s, ch], hs.at[ch, d], hr.at[ch, d], (c, t))

    def mirror(ch, k, e):
        j = rem(c + k, chans)
        m = rem(member + e, 2)
        source = it.at[ch, lines(m, rows), columns(j, width)]
        target = mt.at[slot, ch]
        n = k * 2 + e
        if n == 0:
            return pltpu.make_async_copy(source, target, lm.at[ch])
        return remote(source, target, ms.at[ch, n], mr.at[ch, n], (j, group * 2 + m))

    def deliver(source, ch, u):
        j = u // 2
        p = rem(u, 2)
        away = rem(j - c + chans, chans)
        target = dd.at[p * chans + c, ch]

        @pl.when(away == 0)
        def _():
            pltpu.make_async_copy(source, target, lf.at[ch, p]).start()

        @pl.when(away != 0)
        def _():
            n = away * 2 + p
            remote(source, target, fs.at[ch, n], fr.at[ch, n], (j, s)).start()

    load = pltpu.make_async_copy(r, rf, lv.at[0])
    load.start()

    def send(ch, carry):
        if first:
            for d in range(strips):
                along(ch, d).start()
            for k in range(chans):
                for p in range(2):
                    across(ch, k, p).start()
        else:
            for k in range(1, chans):
                for p in range(2):
                    across(ch, k, p).start()
            for p in range(2):
                relay(v.at[p * chans + c, ch], ch, c * 2 + p)
        return carry

    lax.fori_loop(0, per, send, 0)

    load.wait()
    step = grid // 8

    def split(n, carry):
        part = lines(n, step)
        whole = rf[part, :]
        high = whole.astype(jnp.bfloat16)
        rhi[part, :] = high
        rlo[part, :] = (whole - high.astype(jnp.float32)).astype(jnp.bfloat16)
        return carry

    lax.fori_loop(0, 8, split, 0)

    if not first:

        def pass_on(ch, carry):
            for k in range(1, chans):
                j = rem(c - k + chans, chans)
                for p in range(2):
                    across(ch, k, p).wait_recv()
                    relay(extra.at[p * chans + j, ch], ch, j * 2 + p)
            return carry

        lax.fori_loop(0, per, pass_on, 0)

    tile = 256 if grid % 256 == 0 else 128

    def product(ch, carry):
        along(ch, 0).wait()
        for d in range(1, strips):
            along(ch, d).wait_recv()
        fetch = pltpu.make_async_copy(y.at[ch], vf, lv.at[0])
        fetch.start()
        fetch.wait()

        def cut(n, inner):
            part = lines(n, step)
            whole = vf[part, :]
            high = whole.astype(jnp.bfloat16)
            vhi[part, :] = high
            vlo[part, :] = (whole - high.astype(jnp.float32)).astype(jnp.bfloat16)
            return inner

        lax.fori_loop(0, 8, cut, 0)

        def block(n, inner):
            part = lines(n, tile)
            high = rhi[part, :]
            total = jnp.dot(high, vhi[...], preferred_element_type=jnp.float32)
            total += jnp.dot(high, vlo[...], preferred_element_type=jnp.float32)
            total += jnp.dot(rlo[part, :], vhi[...], preferred_element_type=jnp.float32)
            ibuf[part, :] = total
            tbuf[:, columns(n, tile)] = total.T
            return inner

        lax.fori_loop(0, grid // tile, block, 0)
        out = [
            pltpu.make_async_copy(ibuf, i.at[ch], lv.at[1]),
            pltpu.make_async_copy(tbuf, it.at[ch], lv.at[2]),
        ]
        for copy in out:
            copy.start()
        for copy in out:
            copy.wait()
        for d in range(1, strips):
            back(ch, d).start()
        for k in range(chans):
            for e in range(2):
                mirror(ch, k, e).start()
        deliver(i.at[ch, lines(s, rows), :], ch, s)
        return carry

    lax.fori_loop(0, per, product, 0)

    def finish(ch, carry):
        for d in range(1, strips):
            back(ch, d).wait_recv()
            u = rem(s - d + strips, strips)
            deliver(w.at[u, ch], ch, u)
        return carry

    lax.fori_loop(0, per, finish, 0)

    def drain(ch, carry):
        for d in range(1, strips):
            along(ch, d).wait_send()
            back(ch, d).wait_send()
        for k in range(chans):
            for p in range(2):
                mirror(ch, k, p).wait()
                if first:
                    across(ch, k, p).wait()
                elif k > 0:
                    across(ch, k, p).wait_send()
                source = w.at[0, ch]
                target = dd.at[p * chans + rem(c - k + chans, chans), ch]
                if k == 0:
                    pltpu.make_async_copy(source, target, lf.at[ch, p]).wait()
                else:
                    n = k * 2 + p
                    remote(
                        source, target, fs.at[ch, n], fr.at[ch, n], (rem(c + k, chans), s)
                    ).wait()
        return carry

    lax.fori_loop(0, per, drain, 0)


def apply_radial(first, field, radial_op, tiles):
    chans = lax.axis_size("chan")
    strips = lax.axis_size("strip")
    per, rows, width = tiles[1:]
    grid = radial_op.shape[0]
    tall = (per, grid, width)
    turned = (per, width, grid)
    outs = [tiles, tall, tall, turned, (strips, per, rows, width), tiles, tiles]
    dma = pltpu.SemaphoreType.DMA
    pairs = (per, 2 * chans)
    around = (per, strips)
    scratch = [
        pltpu.VMEM((grid, grid), jnp.float32),
        pltpu.VMEM((grid, grid), jnp.bfloat16),
        pltpu.VMEM((grid, grid), jnp.bfloat16),
        pltpu.VMEM((grid, width), jnp.float32),
        pltpu.VMEM((grid, width), jnp.bfloat16),
        pltpu.VMEM((grid, width), jnp.bfloat16),
        pltpu.VMEM((grid, width), jnp.float32),
        pltpu.VMEM((width, grid), jnp.float32),
    ]
    sems = [pairs, pairs, around, around, around, around, pairs, pairs, pairs, pairs]
    sems = sems + [(per,), (per, 2), (per,), (per, 2), (3,)]
    result = pl.pallas_call(
        functools.partial(apply_kernel, first, chans, strips),
        out_shape=[jax.ShapeDtypeStruct(shape, jnp.float32) for shape in outs],
        in_specs=[ANY] * 2,
        out_specs=[ANY] * len(outs),
        scratch_shapes=scratch + [dma(n) for n in sems],
        compiler_params=pltpu.CompilerParams(
            collective_id=0 if first else 1, has_side_effects=True, vmem_limit_bytes=60 * 2**20
        ),
    )(field, radial_op)
    return result[0], result[6], result[5]


def couple_kernel(count, last, ints, reals, *refs):
    if last:
        field, direct, mirror, base, out, pots = refs
    else:
        field, direct, mirror, out, pots = refs
    channels, height, width = field.shape[1:]
    orders = pots.shape[0]
    spacing = 8.0 / count
    row = ints[0] + pl.program_id(0) * height
    row = row + lax.broadcasted_iota(jnp.int32, (height, width), 0)
    col = ints[1] + lax.broadcasted_iota(jnp.int32, (height, width), 1)
    first = row.astype(jnp.float32) * spacing
    second = col.astype(jnp.float32) * spacing
    greater = jnp.maximum(first, second)
    root = jnp.sqrt(greater * greater + 1.0)
    ratio = jnp.minimum(first, second) / root
    pot = 1.0 / root
    for order in range(orders):
        pots[order] = pot
        pot = pot * ratio
    reach = jnp.maximum(row, col)

    def channel(c, carry):
        other = ints[2 + c]
        real_part = direct[0, c] + mirror[0, other]
        imag_part = direct[1, c] + mirror[1, other]
        for order in range(orders):
            k = ints[2 + 2 * channels + c * orders + order]
            c_real = reals[c * orders + order]
            c_imag = reals[channels * orders + c * orders + order]
            pot = pots[order]
            s_real = pot * field[0, k]
            s_imag = pot * field[1, k]
            real_part = real_part + (c_real * s_real - c_imag * s_imag)
            imag_part = imag_part + (c_real * s_imag + c_imag * s_real)
        live = reach < ints[2 + channels + c]
        real_part = jnp.where(live, real_part, 0.0)
        imag_part = jnp.where(live, imag_part, 0.0)
        if last:
            real_part = 2.0 * real_part - base[0, c]
            imag_part = 2.0 * imag_part - base[1, c]
        out[0, c] = real_part
        out[1, c] = imag_part
        return carry

    lax.fori_loop(0, channels, channel, 0)


def couple_tiles(count, ints, reals, orders, arrays):
    last = len(arrays) == 4
    shape = arrays[0].shape
    height = 16
    block = pl.BlockSpec((2, shape[1], height, shape[3]), lambda n: (0, 0, n, 0))
    smem = pl.BlockSpec(memory_space=pltpu.SMEM)
    return pl.pallas_call(
        functools.partial(couple_kernel, count, last),
        grid=(shape[2] // height,),
        out_shape=jax.ShapeDtypeStruct(shape, jnp.float32),
        in_specs=[smem, smem] + [block] * len(arrays),
        out_specs=block,
        scratch_shapes=[pltpu.VMEM((orders, height, shape[3]), jnp.float32)],
    )(ints, reals, *arrays)


def local(wave_field, radial_op, coupling, couple, partner, extent):
    chans = lax.axis_size("chan")
    strips = lax.axis_size("strip")
    per, rows, grid = wave_field.shape[1:]
    width = grid // chans
    orders = coupling.shape[2]
    tiles = (2 * chans, per, rows, width)
    whole = (2, chans * per, rows, width)
    starts = jnp.stack([lax.axis_index("strip") * rows, lax.axis_index("chan") * width])
    ints = jnp.concatenate([starts.astype(jnp.int32), partner, extent, couple.reshape(-1)])
    reals = coupling.reshape(-1)
    flat = wave_field.reshape(2 * per, rows, grid)
    parts = [part.reshape(whole) for part in apply_radial(True, flat, radial_op, tiles)]
    field = parts[0]
    first_step = couple_tiles(grid, ints, reals, orders, parts)
    parts = apply_radial(False, first_step.reshape(tiles), radial_op, tiles)[1:]
    parts = [first_step] + [part.reshape(whole) for part in parts] + [field]
    second_step = couple_tiles(grid, ints, reals, orders, parts)
    return (first_step, second_step)


def dispatch(wave_field, *rest):
    chans = lax.axis_size("chan")
    strips = lax.axis_size("strip")
    width = wave_field.shape[3] // chans
    if strips == 2 * chans and width % 128 == 0 and wave_field.shape[2] % 16 == 0:
        return local(wave_field, *rest)
    return general(wave_field, *rest)


def solution(mesh):
    placed = (P(None, "chan", "strip", None), P(), P(), P(), P(), P())
    return jax.shard_map(
        dispatch,
        mesh=mesh,
        in_specs=placed,
        out_specs=(P(None, None, "strip", "chan"), P(None, None, "strip", "chan")),
        check_vma=False,
    )
```

```python
import functools

import jax
import jax.numpy as jnp
from jax import lax
from jax.experimental import pallas as pl
from jax.experimental.pallas import tpu as pltpu
from jax.sharding import PartitionSpec as P


def potentials(row_pos, col_pos, count, orders):
    spacing = 8.0 / count
    first = row_pos.astype(jnp.float32) * spacing
    second = col_pos.astype(jnp.float32) * spacing
    lesser = jnp.minimum(first[:, None], second[None, :])
    greater = jnp.maximum(first[:, None], second[None, :])
    root = jnp.sqrt(greater * greater + 1.0)
    result = []
    for order in range(orders):
        result.append(lesser**order / root ** (order + 1))
    return result


def couple_terms(field, image_rows, mirrored, coupling, couple, partner, pots, live):
    total = image_rows + jnp.take(mirrored, partner, axis=1)
    real_part = total[0]
    imag_part = total[1]
    for order in range(len(pots)):
        source = jnp.take(field, couple[:, order], axis=1)
        c_real = coupling[0, :, order][:, None, None]
        c_imag = coupling[1, :, order][:, None, None]
        real_part = real_part + pots[order] * (c_real * source[0] - c_imag * source[1])
        imag_part = imag_part + pots[order] * (c_real * source[1] + c_imag * source[0])
    return jnp.where(live[None], jnp.stack([real_part, imag_part]), 0.0)


def radial_product(radial_op, block):
    return jnp.einsum("ak,pckb->pcab", radial_op, block, precision=lax.Precision.HIGHEST)


def spread_columns(field):
    strips = lax.axis_size("strip")
    local_chans = field.shape[1]
    local_rows = field.shape[2]
    grid = field.shape[3]
    piece = grid // (strips * strips)
    shaped = field.reshape(2, local_chans, local_rows, strips, strips, piece)
    return jnp.transpose(shaped, (0, 1, 2, 4, 3, 5)).reshape(2, local_chans, local_rows, grid)


def spread_tiles(image):
    chans = lax.axis_size("chan")
    strips = lax.axis_size("strip")
    local_chans = image.shape[1]
    grid = image.shape[2]
    width = image.shape[3]
    piece = grid // (strips * strips)
    ratio = strips // chans
    block = grid // chans
    direct_send = image.reshape(2, local_chans, strips, width, chans, ratio * piece)
    direct_send = jnp.transpose(direct_send, (0, 1, 4, 2, 3, 5)).reshape(
        2, local_chans, chans * strips, width, ratio * piece
    )
    mirror_send = image.reshape(2, local_chans, chans, block, strips, piece)
    mirror_send = jnp.transpose(mirror_send, (0, 1, 2, 4, 3, 5)).reshape(
        2, local_chans, chans * strips, block, piece
    )
    direct_got, mirror_got = (
        lax.all_to_all(direct_send, ("chan", "strip"), split_axis=2, concat_axis=2, tiled=True),
        lax.all_to_all(mirror_send, ("chan", "strip"), split_axis=2, concat_axis=2, tiled=True),
    )
    direct_got = direct_got.reshape(2, local_chans, chans, strips, width, ratio, piece)
    direct_tiles = jnp.transpose(direct_got, (0, 2, 1, 4, 5, 3, 6)).reshape(
        2, chans * local_chans, width, block
    )
    mirror_got = mirror_got.reshape(2, local_chans, chans, strips, block, piece)
    mirror_tiles = jnp.transpose(mirror_got, (0, 2, 1, 3, 5, 4)).reshape(
        2, chans * local_chans, width, block
    )
    return (direct_tiles, mirror_tiles)


def general(wave_field, radial_op, coupling, couple, partner, extent):
    chans = lax.axis_size("chan")
    grid = wave_field.shape[3]
    strip_rows = wave_field.shape[2]
    chan_cols = grid // chans
    row_pos = lax.axis_index("strip") * strip_rows + jnp.arange(strip_rows)
    col_pos = lax.axis_index("chan") * chan_cols + jnp.arange(chan_cols)
    pots = potentials(row_pos, col_pos, grid, coupling.shape[2])
    live = (row_pos[None, :, None] < extent[:, None, None]) & (
        col_pos[None, None, :] < extent[:, None, None]
    )

    def radial(block):
        return radial_product(radial_op, block)

    def product_columns(field_rows):
        return radial(lax.all_to_all(field_rows, "strip", split_axis=3, concat_axis=2, tiled=True))

    field_tiles = lax.all_to_all(wave_field, "chan", split_axis=3, concat_axis=1, tiled=True)
    rows_tiles, mirror_tiles = spread_tiles(product_columns(spread_columns(wave_field)))
    first_step = couple_terms(
        field_tiles, rows_tiles, mirror_tiles, coupling, couple, partner, pots, live
    )
    image = product_columns(
        spread_columns(lax.all_to_all(first_step, "chan", split_axis=1, concat_axis=3, tiled=True))
    )
    rows_tiles, mirror_tiles = spread_tiles(image)
    applied = couple_terms(
        first_step, rows_tiles, mirror_tiles, coupling, couple, partner, pots, live
    )
    second_step = 2.0 * applied - field_tiles
    return (first_step, second_step)


MESH = pl.DeviceIdType.MESH
ANY = pl.BlockSpec(memory_space=pl.ANY)


def rem(value, count):
    return lax.rem(value, count)


def greet(others):
    barrier = pltpu.get_barrier_semaphore()
    for other in others:
        pl.semaphore_signal(barrier, inc=1, device_id=other, device_id_type=MESH)
    pl.semaphore_wait(barrier, len(others))


def remote(source, target, send, recv, device):
    return pltpu.make_async_remote_copy(
        src_ref=source,
        dst_ref=target,
        send_sem=send,
        recv_sem=recv,
        device_id=device,
        device_id_type=MESH,
    )


def columns(block, width):
    return pl.ds(pl.multiple_of(block * width, 128), width)


def lines(block, height):
    return pl.ds(pl.multiple_of(block * height, 8), height)


def apply_kernel(first, chans, strips, *refs):
    head = 11 if first else 7
    if first:
        v, r, i, it, w, mt, dd, extra, y, yt, ft = refs[:head]
    else:
        v, r, i, it, w, mt, dd, ut = refs[: head + 1]
        head = head + 1
    rf, rhi, rlo, vf, vhi, vlo, ibuf, tbuf = refs[head : head + 8]
    cs, cr, zs, zr, hs, hr, ms, mr, fs, fr, ts, tr, lz, lc, lm, lf, lt, lv = refs[head + 8 :]
    c = lax.axis_index("chan")
    s = lax.axis_index("strip")
    per, grid, width = i.shape
    rows = w.shape[2]
    group = s // 2
    member = rem(s, 2)
    slot = member * chans + c
    greet(
        [(c, rem(s + d, strips)) for d in range(1, strips)]
        + [(rem(c + k, chans), s) for k in range(1, chans)]
        + [(rem(c + k, chans), group * 2 + rem(member + 1, 2)) for k in range(1, chans)]
    )

    def across(ch, k, p):
        j = rem(c + k, chans)
        source = v.at[p * per + ch, :, columns(j, width)]
        target = extra.at[p * chans + c, ch]
        if k == 0:
            return pltpu.make_async_copy(source, target, lc.at[ch, p])
        n = k * 2 + p
        return remote(source, target, cs.at[ch, n], cr.at[ch, n], (j, s))

    def along(ch, d):
        t = rem(s + d, strips)
        source = v.at[rem(t, 2) * per + ch, :, columns(t // 2, width)]
        target = y.at[ch, lines(s, rows), :]
        if d == 0:
            return pltpu.make_async_copy(source, target, lz.at[ch])
        return remote(source, target, zs.at[ch, d], zr.at[ch, d], (c, t))

    def regroup(ch, k, e):
        j = rem(c + k, chans)
        p = rem(member + e, 2)
        source = v.at[p * chans + j, ch]
        target = ut.at[ch, lines(member, rows), columns(c, width)]
        n = k * 2 + e
        if n == 0:
            return pltpu.make_async_copy(source, target, lt.at[ch])
        return remote(source, target, ts.at[ch, n], tr.at[ch, n], (j, group * 2 + p))

    def turn(ch, k, e):
        j = rem(c + k, chans)
        m = rem(member + e, 2)
        source = yt.at[ch, lines(m, rows), columns(j, width)]
        target = ft.at[slot, ch]
        n = k * 2 + e
        if n == 0:
            return pltpu.make_async_copy(source, target, lt.at[ch])
        return remote(source, target, ts.at[ch, n], tr.at[ch, n], (j, group * 2 + m))

    def back(ch, d):
        t = rem(s + d, strips)
        source = i.at[ch, lines(t, rows), :]
        return remote(source, w.at[s, ch], hs.at[ch, d], hr.at[ch, d], (c, t))

    def mirror(ch, k, e):
        j = rem(c + k, chans)
        m = rem(member + e, 2)
        source = it.at[ch, lines(m, rows), columns(j, width)]
        target = mt.at[slot, ch]
        n = k * 2 + e
        if n == 0:
            return pltpu.make_async_copy(source, target, lm.at[ch])
        return remote(source, target, ms.at[ch, n], mr.at[ch, n], (j, group * 2 + m))

    def deliver(source, ch, u):
        j = u // 2
        p = rem(u, 2)
        away = rem(j - c + chans, chans)
        target = dd.at[p * chans + c, ch]

        @pl.when(away == 0)
        def _():
            pltpu.make_async_copy(source, target, lf.at[ch, p]).start()

        @pl.when(away != 0)
        def _():
            n = away * 2 + p
            remote(source, target, fs.at[ch, n], fr.at[ch, n], (j, s)).start()

    load = pltpu.make_async_copy(r, rf, lv.at[0])
    load.start()

    def send(ch, carry):
        if first:
            for d in range(strips):
                along(ch, d).start()
            for k in range(chans):
                for p in range(2):
                    across(ch, k, p).start()
        else:
            for k in range(chans):
                for e in range(2):
                    regroup(ch, k, e).start()
        return carry

    lax.fori_loop(0, per, send, 0)

    load.wait()
    step = grid // 8

    def split(n, carry):
        part = lines(n, step)
        whole = rf[part, :]
        high = whole.astype(jnp.bfloat16)
        rhi[part, :] = high
        rlo[part, :] = (whole - high.astype(jnp.float32)).astype(jnp.bfloat16)
        return carry

    lax.fori_loop(0, 8, split, 0)

    tile = 256 if grid % 256 == 0 else 128

    def product(ch, carry):
        if first:
            along(ch, 0).wait()
            for d in range(1, strips):
                along(ch, d).wait_recv()
        else:
            regroup(ch, 0, 0).wait()
            for n in range(1, 2 * chans):
                regroup(ch, n // 2, n % 2).wait_recv()
        fetch = pltpu.make_async_copy((y if first else ut).at[ch], vf, lv.at[0])
        fetch.start()
        fetch.wait()
        length = vf.shape[0] // 8

        def cut(n, inner):
            part = lines(n, length)
            whole = vf[part, :]
            high = whole.astype(jnp.bfloat16)
            vhi[part, :] = high
            vlo[part, :] = (whole - high.astype(jnp.float32)).astype(jnp.bfloat16)
            return inner

        lax.fori_loop(0, 8, cut, 0)

        if first:

            def flip(n, inner):
                tbuf[:, columns(n, tile)] = vf[lines(n, tile), :].T
                return inner

            lax.fori_loop(0, grid // tile, flip, 0)
            copy = pltpu.make_async_copy(tbuf, yt.at[ch], lv.at[2])
            copy.start()
            copy.wait()
            for k in range(chans):
                for e in range(2):
                    turn(ch, k, e).start()

        def block(n, inner):
            part = lines(n, tile)
            if first:
                pairs = [(rhi[part, :], vhi), (rhi[part, :], vlo), (rlo[part, :], vhi)]
                pairs = [(left, right[...]) for left, right in pairs]
            else:
                high = rhi[:, columns(n, tile)]
                pairs = [(vhi[...], high), (vlo[...], high), (vhi[...], rlo[:, columns(n, tile)])]
            total = None
            for left, right in pairs:
                term = jnp.dot(left, right, preferred_element_type=jnp.float32)
                total = term if total is None else total + term
            if first:
                ibuf[part, :] = total
                tbuf[:, columns(n, tile)] = total.T
            else:
                ibuf[part, :] = total.T
                tbuf[:, columns(n, tile)] = total
            return inner

        lax.fori_loop(0, grid // tile, block, 0)
        out = [
            pltpu.make_async_copy(ibuf, i.at[ch], lv.at[1]),
            pltpu.make_async_copy(tbuf, it.at[ch], lv.at[2]),
        ]
        for copy in out:
            copy.start()
        for copy in out:
            copy.wait()
        for d in range(1, strips):
            back(ch, d).start()
        for k in range(chans):
            for e in range(2):
                mirror(ch, k, e).start()
        deliver(i.at[ch, lines(s, rows), :], ch, s)
        return carry

    lax.fori_loop(0, per, product, 0)

    def finish(ch, carry):
        for d in range(1, strips):
            back(ch, d).wait_recv()
            u = rem(s - d + strips, strips)
            deliver(w.at[u, ch], ch, u)
        return carry

    lax.fori_loop(0, per, finish, 0)

    def drain(ch, carry):
        for d in range(1, strips):
            if first:
                along(ch, d).wait_send()
            back(ch, d).wait_send()
        for k in range(chans):
            for p in range(2):
                mirror(ch, k, p).wait()
                if first:
                    across(ch, k, p).wait()
                    turn(ch, k, p).wait()
                elif k + p > 0:
                    regroup(ch, k, p).wait_send()
                source = w.at[0, ch]
                target = dd.at[p * chans + rem(c - k + chans, chans), ch]
                if k == 0:
                    pltpu.make_async_copy(source, target, lf.at[ch, p]).wait()
                else:
                    n = k * 2 + p
                    remote(
                        source, target, fs.at[ch, n], fr.at[ch, n], (rem(c + k, chans), s)
                    ).wait()
        return carry

    lax.fori_loop(0, per, drain, 0)


def apply_radial(first, field, radial_op, tiles):
    chans = lax.axis_size("chan")
    strips = lax.axis_size("strip")
    per, rows, width = tiles[1:]
    grid = radial_op.shape[0]
    tall = (per, grid, width)
    turned = (per, width, grid)
    outs = [tall, turned, (strips, per, rows, width), tiles, tiles]
    outs = outs + ([tiles, tall, turned, tiles] if first else [turned])
    held = tall if first else turned
    dma = pltpu.SemaphoreType.DMA
    pairs = (per, 2 * chans)
    around = (per, strips)
    scratch = [
        pltpu.VMEM((grid, grid), jnp.float32),
        pltpu.VMEM((grid, grid), jnp.bfloat16),
        pltpu.VMEM((grid, grid), jnp.bfloat16),
        pltpu.VMEM(held[1:], jnp.float32),
        pltpu.VMEM(held[1:], jnp.bfloat16),
        pltpu.VMEM(held[1:], jnp.bfloat16),
        pltpu.VMEM(tall[1:], jnp.float32),
        pltpu.VMEM((width, grid), jnp.float32),
    ]
    sems = [pairs] * 2 + [around] * 4 + [pairs] * 6
    sems = sems + [(per,), (per, 2), (per,), (per, 2), (per,), (3,)]
    result = pl.pallas_call(
        functools.partial(apply_kernel, first, chans, strips),
        out_shape=[jax.ShapeDtypeStruct(shape, jnp.float32) for shape in outs],
        in_specs=[ANY] * 2,
        out_specs=[ANY] * len(outs),
        scratch_shapes=scratch + [dma(n) for n in sems],
        compiler_params=pltpu.CompilerParams(
            collective_id=0 if first else 1, has_side_effects=True, vmem_limit_bytes=60 * 2**20
        ),
    )(field, radial_op)
    if first:
        return result[5], result[8], result[4], result[3]
    return result[4], result[3]


def couple_kernel(count, last, ints, reals, *refs):
    if last:
        field, direct, mirror, base, out, pots = refs
    else:
        field, direct, mirror, out, pots = refs
    channels, height, width = field.shape[1:]
    orders = pots.shape[0]
    spacing = 8.0 / count
    row = ints[0] + pl.program_id(0) * height
    row = row + lax.broadcasted_iota(jnp.int32, (height, width), 0)
    col = ints[1] + lax.broadcasted_iota(jnp.int32, (height, width), 1)
    first = row.astype(jnp.float32) * spacing
    second = col.astype(jnp.float32) * spacing
    greater = jnp.maximum(first, second)
    root = jnp.sqrt(greater * greater + 1.0)
    ratio = jnp.minimum(first, second) / root
    pot = 1.0 / root
    for order in range(orders):
        pots[order] = pot
        pot = pot * ratio
    reach = jnp.maximum(row, col)

    def channel(c, carry):
        other = ints[2 + c]
        real_part = direct[0, c] + mirror[0, other]
        imag_part = direct[1, c] + mirror[1, other]
        for order in range(orders):
            k = ints[2 + 2 * channels + c * orders + order]
            c_real = reals[c * orders + order]
            c_imag = reals[channels * orders + c * orders + order]
            pot = pots[order]
            s_real = pot * field[0, k]
            s_imag = pot * field[1, k]
            real_part = real_part + (c_real * s_real - c_imag * s_imag)
            imag_part = imag_part + (c_real * s_imag + c_imag * s_real)
        live = reach < ints[2 + channels + c]
        real_part = jnp.where(live, real_part, 0.0)
        imag_part = jnp.where(live, imag_part, 0.0)
        if last:
            real_part = 2.0 * real_part - base[0, c]
            imag_part = 2.0 * imag_part - base[1, c]
        out[0, c] = real_part
        out[1, c] = imag_part
        return carry

    lax.fori_loop(0, channels, channel, 0)


def couple_tiles(count, ints, reals, orders, arrays):
    last = len(arrays) == 4
    shape = arrays[0].shape
    height = 16
    block = pl.BlockSpec((2, shape[1], height, shape[3]), lambda n: (0, 0, n, 0))
    smem = pl.BlockSpec(memory_space=pltpu.SMEM)
    return pl.pallas_call(
        functools.partial(couple_kernel, count, last),
        grid=(shape[2] // height,),
        out_shape=jax.ShapeDtypeStruct(shape, jnp.float32),
        in_specs=[smem, smem] + [block] * len(arrays),
        out_specs=block,
        scratch_shapes=[pltpu.VMEM((orders, height, shape[3]), jnp.float32)],
    )(ints, reals, *arrays)


def local(wave_field, radial_op, coupling, couple, partner, extent):
    chans = lax.axis_size("chan")
    strips = lax.axis_size("strip")
    per, rows, grid = wave_field.shape[1:]
    width = grid // chans
    orders = coupling.shape[2]
    tiles = (2 * chans, per, rows, width)
    whole = (2, chans * per, rows, width)
    starts = jnp.stack([lax.axis_index("strip") * rows, lax.axis_index("chan") * width])
    ints = jnp.concatenate([starts.astype(jnp.int32), partner, extent, couple.reshape(-1)])
    reals = coupling.reshape(-1)
    flat = wave_field.reshape(2 * per, rows, grid)
    parts = [part.reshape(whole) for part in apply_radial(True, flat, radial_op, tiles)]
    field, turned, direct, mirror = parts
    first_turned = couple_tiles(grid, ints, reals, orders, (turned, mirror, direct))
    first_step = couple_tiles(grid, ints, reals, orders, (field, direct, mirror))
    parts = apply_radial(False, first_turned.reshape(tiles), radial_op, tiles)
    parts = [first_step] + [part.reshape(whole) for part in parts] + [field]
    second_step = couple_tiles(grid, ints, reals, orders, parts)
    return (first_step, second_step)


def dispatch(wave_field, *rest):
    chans = lax.axis_size("chan")
    strips = lax.axis_size("strip")
    width = wave_field.shape[3] // chans
    if strips == 2 * chans and width % 128 == 0 and wave_field.shape[2] % 16 == 0:
        return local(wave_field, *rest)
    return general(wave_field, *rest)


def solution(mesh):
    placed = (P(None, "chan", "strip", None), P(), P(), P(), P(), P())
    return jax.shard_map(
        dispatch,
        mesh=mesh,
        in_specs=placed,
        out_specs=(P(None, None, "strip", "chan"), P(None, None, "strip", "chan")),
        check_vma=False,
    )
```

```python
import functools

import jax
import jax.numpy as jnp
from jax import lax
from jax.experimental import pallas as pl
from jax.experimental.pallas import tpu as pltpu
from jax.sharding import PartitionSpec as P


def potentials(row_pos, col_pos, count, orders):
    spacing = 8.0 / count
    first = row_pos.astype(jnp.float32) * spacing
    second = col_pos.astype(jnp.float32) * spacing
    lesser = jnp.minimum(first[:, None], second[None, :])
    greater = jnp.maximum(first[:, None], second[None, :])
    root = jnp.sqrt(greater * greater + 1.0)
    result = []
    for order in range(orders):
        result.append(lesser**order / root ** (order + 1))
    return result


def couple_terms(field, image_rows, mirrored, coupling, couple, partner, pots, live):
    total = image_rows + jnp.take(mirrored, partner, axis=1)
    real_part = total[0]
    imag_part = total[1]
    for order in range(len(pots)):
        source = jnp.take(field, couple[:, order], axis=1)
        c_real = coupling[0, :, order][:, None, None]
        c_imag = coupling[1, :, order][:, None, None]
        real_part = real_part + pots[order] * (c_real * source[0] - c_imag * source[1])
        imag_part = imag_part + pots[order] * (c_real * source[1] + c_imag * source[0])
    return jnp.where(live[None], jnp.stack([real_part, imag_part]), 0.0)


def radial_product(radial_op, block):
    return jnp.einsum("ak,pckb->pcab", radial_op, block, precision=lax.Precision.HIGHEST)


def spread_columns(field):
    strips = lax.axis_size("strip")
    local_chans = field.shape[1]
    local_rows = field.shape[2]
    grid = field.shape[3]
    piece = grid // (strips * strips)
    shaped = field.reshape(2, local_chans, local_rows, strips, strips, piece)
    return jnp.transpose(shaped, (0, 1, 2, 4, 3, 5)).reshape(2, local_chans, local_rows, grid)


def spread_tiles(image):
    chans = lax.axis_size("chan")
    strips = lax.axis_size("strip")
    local_chans = image.shape[1]
    grid = image.shape[2]
    width = image.shape[3]
    piece = grid // (strips * strips)
    ratio = strips // chans
    block = grid // chans
    direct_send = image.reshape(2, local_chans, strips, width, chans, ratio * piece)
    direct_send = jnp.transpose(direct_send, (0, 1, 4, 2, 3, 5)).reshape(
        2, local_chans, chans * strips, width, ratio * piece
    )
    mirror_send = image.reshape(2, local_chans, chans, block, strips, piece)
    mirror_send = jnp.transpose(mirror_send, (0, 1, 2, 4, 3, 5)).reshape(
        2, local_chans, chans * strips, block, piece
    )
    direct_got, mirror_got = (
        lax.all_to_all(direct_send, ("chan", "strip"), split_axis=2, concat_axis=2, tiled=True),
        lax.all_to_all(mirror_send, ("chan", "strip"), split_axis=2, concat_axis=2, tiled=True),
    )
    direct_got = direct_got.reshape(2, local_chans, chans, strips, width, ratio, piece)
    direct_tiles = jnp.transpose(direct_got, (0, 2, 1, 4, 5, 3, 6)).reshape(
        2, chans * local_chans, width, block
    )
    mirror_got = mirror_got.reshape(2, local_chans, chans, strips, block, piece)
    mirror_tiles = jnp.transpose(mirror_got, (0, 2, 1, 3, 5, 4)).reshape(
        2, chans * local_chans, width, block
    )
    return (direct_tiles, mirror_tiles)


def general(wave_field, radial_op, coupling, couple, partner, extent):
    chans = lax.axis_size("chan")
    grid = wave_field.shape[3]
    strip_rows = wave_field.shape[2]
    chan_cols = grid // chans
    row_pos = lax.axis_index("strip") * strip_rows + jnp.arange(strip_rows)
    col_pos = lax.axis_index("chan") * chan_cols + jnp.arange(chan_cols)
    pots = potentials(row_pos, col_pos, grid, coupling.shape[2])
    live = (row_pos[None, :, None] < extent[:, None, None]) & (
        col_pos[None, None, :] < extent[:, None, None]
    )

    def radial(block):
        return radial_product(radial_op, block)

    def product_columns(field_rows):
        return radial(lax.all_to_all(field_rows, "strip", split_axis=3, concat_axis=2, tiled=True))

    field_tiles = lax.all_to_all(wave_field, "chan", split_axis=3, concat_axis=1, tiled=True)
    rows_tiles, mirror_tiles = spread_tiles(product_columns(spread_columns(wave_field)))
    first_step = couple_terms(
        field_tiles, rows_tiles, mirror_tiles, coupling, couple, partner, pots, live
    )
    image = product_columns(
        spread_columns(lax.all_to_all(first_step, "chan", split_axis=1, concat_axis=3, tiled=True))
    )
    rows_tiles, mirror_tiles = spread_tiles(image)
    applied = couple_terms(
        first_step, rows_tiles, mirror_tiles, coupling, couple, partner, pots, live
    )
    second_step = 2.0 * applied - field_tiles
    return (first_step, second_step)


MESH = pl.DeviceIdType.MESH
ANY = pl.BlockSpec(memory_space=pl.ANY)


def rem(value, count):
    return lax.rem(value, count)


def greet(others):
    barrier = pltpu.get_barrier_semaphore()
    for other in others:
        pl.semaphore_signal(barrier, inc=1, device_id=other, device_id_type=MESH)
    pl.semaphore_wait(barrier, len(others))


def remote(source, target, send, recv, device):
    return pltpu.make_async_remote_copy(
        src_ref=source,
        dst_ref=target,
        send_sem=send,
        recv_sem=recv,
        device_id=device,
        device_id_type=MESH,
    )


def columns(block, width):
    return pl.ds(pl.multiple_of(block * width, 128), width)


def lines(block, height):
    return pl.ds(pl.multiple_of(block * height, 8), height)


def apply_kernel(first, chans, strips, *refs):
    head = 11 if first else 7
    if first:
        v, r, i, it, w, mt, dd, extra, y, yt, ft = refs[:head]
    else:
        v, r, i, it, w, mt, dd, ut = refs[: head + 1]
        head = head + 1
    rf, rhi, rlo, vf, vhi, vlo, ibuf, tbuf = refs[head : head + 8]
    cs, cr, zs, zr, hs, hr, ms, mr, fs, fr, ts, tr, lz, lc, lm, lf, lt, lv = refs[head + 8 :]
    c = lax.axis_index("chan")
    s = lax.axis_index("strip")
    per, grid, width = i.shape
    rows = w.shape[2]
    group = s // 2
    member = rem(s, 2)
    slot = member * chans + c
    greet(
        [(c, rem(s + d, strips)) for d in range(1, strips)]
        + [(rem(c + k, chans), s) for k in range(1, chans)]
        + [(rem(c + k, chans), group * 2 + rem(member + 1, 2)) for k in range(1, chans)]
    )

    def across(ch, k, p):
        j = rem(c + k, chans)
        source = v.at[p * per + ch, :, columns(j, width)]
        target = extra.at[p * chans + c, ch]
        if k == 0:
            return pltpu.make_async_copy(source, target, lc.at[ch, p])
        n = k * 2 + p
        return remote(source, target, cs.at[ch, n], cr.at[ch, n], (j, s))

    def along(ch, d):
        t = rem(s + d, strips)
        source = v.at[rem(t, 2) * per + ch, :, columns(t // 2, width)]
        target = y.at[ch, lines(s, rows), :]
        if d == 0:
            return pltpu.make_async_copy(source, target, lz.at[ch])
        return remote(source, target, zs.at[ch, d], zr.at[ch, d], (c, t))

    def regroup(ch, k, e):
        j = rem(c + k, chans)
        p = rem(member + e, 2)
        source = v.at[p * chans + j, ch]
        target = ut.at[ch, lines(member, rows), columns(c, width)]
        n = k * 2 + e
        if n == 0:
            return pltpu.make_async_copy(source, target, lt.at[ch])
        return remote(source, target, ts.at[ch, n], tr.at[ch, n], (j, group * 2 + p))

    def turn(ch, k, e):
        j = rem(c + k, chans)
        m = rem(member + e, 2)
        source = yt.at[ch, lines(m, rows), columns(j, width)]
        target = ft.at[slot, ch]
        n = k * 2 + e
        if n == 0:
            return pltpu.make_async_copy(source, target, lt.at[ch])
        return remote(source, target, ts.at[ch, n], tr.at[ch, n], (j, group * 2 + m))

    def back(ch, d):
        t = rem(s + d, strips)
        source = i.at[ch, lines(t, rows), :]
        return remote(source, w.at[s, ch], hs.at[ch, d], hr.at[ch, d], (c, t))

    def mirror(ch, k, e):
        j = rem(c + k, chans)
        m = rem(member + e, 2)
        source = it.at[ch, lines(m, rows), columns(j, width)]
        target = mt.at[slot, ch]
        n = k * 2 + e
        if n == 0:
            return pltpu.make_async_copy(source, target, lm.at[ch])
        return remote(source, target, ms.at[ch, n], mr.at[ch, n], (j, group * 2 + m))

    def deliver(source, ch, u):
        j = u // 2
        p = rem(u, 2)
        away = rem(j - c + chans, chans)
        target = dd.at[p * chans + c, ch]

        @pl.when(away == 0)
        def _():
            pltpu.make_async_copy(source, target, lf.at[ch, p]).start()

        @pl.when(away != 0)
        def _():
            n = away * 2 + p
            remote(source, target, fs.at[ch, n], fr.at[ch, n], (j, s)).start()

    load = pltpu.make_async_copy(r, rf, lv.at[0])
    load.start()

    def send(ch, carry):
        if first:
            for d in range(strips):
                along(ch, d).start()
            for k in range(chans):
                for p in range(2):
                    across(ch, k, p).start()
        else:
            for k in range(chans):
                for e in range(2):
                    regroup(ch, k, e).start()
        return carry

    lax.fori_loop(0, per, send, 0)

    load.wait()
    step = grid // 8

    def split(n, carry):
        part = lines(n, step)
        whole = rf[part, :]
        high = whole.astype(jnp.bfloat16)
        rhi[part, :] = high
        rlo[part, :] = (whole - high.astype(jnp.float32)).astype(jnp.bfloat16)
        return carry

    lax.fori_loop(0, 8, split, 0)

    tile = 256 if grid % 256 == 0 else 128

    def product(ch, carry):
        if first:
            along(ch, 0).wait()
            for d in range(1, strips):
                along(ch, d).wait_recv()
        else:
            regroup(ch, 0, 0).wait()
            for n in range(1, 2 * chans):
                regroup(ch, n // 2, n % 2).wait_recv()
        fetch = pltpu.make_async_copy((y if first else ut).at[ch], vf, lv.at[0])
        fetch.start()
        fetch.wait()
        length = vf.shape[0] // 8

        def cut(n, inner):
            part = lines(n, length)
            whole = vf[part, :]
            high = whole.astype(jnp.bfloat16)
            vhi[part, :] = high
            vlo[part, :] = (whole - high.astype(jnp.float32)).astype(jnp.bfloat16)
            return inner

        lax.fori_loop(0, 8, cut, 0)

        if first:

            def flip(n, inner):
                tbuf[:, columns(n, tile)] = vf[lines(n, tile), :].T
                return inner

            lax.fori_loop(0, grid // tile, flip, 0)
            copy = pltpu.make_async_copy(tbuf, yt.at[ch], lv.at[2])
            copy.start()
            copy.wait()
            for k in range(chans):
                for e in range(2):
                    turn(ch, k, e).start()

        def block(n, inner):
            part = lines(n, tile)
            if first:
                pairs = [(rhi[part, :], vhi), (rhi[part, :], vlo), (rlo[part, :], vhi)]
                pairs = [(left, right[...]) for left, right in pairs]
            else:
                high = rhi[:, columns(n, tile)]
                pairs = [(vhi[...], high), (vlo[...], high), (vhi[...], rlo[:, columns(n, tile)])]
            total = None
            for left, right in pairs:
                term = jnp.dot(left, right, preferred_element_type=jnp.float32)
                total = term if total is None else total + term
            if first:
                ibuf[part, :] = total
                tbuf[:, columns(n, tile)] = total.T
            else:
                ibuf[part, :] = total.T
                tbuf[:, columns(n, tile)] = total
            return inner

        lax.fori_loop(0, grid // tile, block, 0)
        out = [
            pltpu.make_async_copy(ibuf, i.at[ch], lv.at[1]),
            pltpu.make_async_copy(tbuf, it.at[ch], lv.at[2]),
        ]
        for copy in out:
            copy.start()
        for copy in out:
            copy.wait()
        for d in range(1, strips):
            back(ch, d).start()
        for k in range(chans):
            for e in range(2):
                mirror(ch, k, e).start()
        deliver(i.at[ch, lines(s, rows), :], ch, s)
        return carry

    lax.fori_loop(0, per, product, 0)

    def finish(ch, carry):
        for d in range(1, strips):
            back(ch, d).wait_recv()
            u = rem(s - d + strips, strips)
            deliver(w.at[u, ch], ch, u)
        return carry

    lax.fori_loop(0, per, finish, 0)

    def drain(ch, carry):
        for d in range(1, strips):
            if first:
                along(ch, d).wait_send()
            back(ch, d).wait_send()
        for k in range(chans):
            for p in range(2):
                mirror(ch, k, p).wait()
                if first:
                    across(ch, k, p).wait()
                    turn(ch, k, p).wait()
                elif k + p > 0:
                    regroup(ch, k, p).wait_send()
                source = w.at[0, ch]
                target = dd.at[p * chans + rem(c - k + chans, chans), ch]
                if k == 0:
                    pltpu.make_async_copy(source, target, lf.at[ch, p]).wait()
                else:
                    n = k * 2 + p
                    remote(
                        source, target, fs.at[ch, n], fr.at[ch, n], (rem(c + k, chans), s)
                    ).wait()
        return carry

    lax.fori_loop(0, per, drain, 0)


def apply_radial(first, field, radial_op, tiles):
    chans = lax.axis_size("chan")
    strips = lax.axis_size("strip")
    per, rows, width = tiles[1:]
    grid = radial_op.shape[0]
    tall = (per, grid, width)
    turned = (per, width, grid)
    outs = [tall, turned, (strips, per, rows, width), tiles, tiles]
    outs = outs + ([tiles, tall, turned, tiles] if first else [turned])
    held = tall if first else turned
    dma = pltpu.SemaphoreType.DMA
    pairs = (per, 2 * chans)
    around = (per, strips)
    scratch = [
        pltpu.VMEM((grid, grid), jnp.float32),
        pltpu.VMEM((grid, grid), jnp.bfloat16),
        pltpu.VMEM((grid, grid), jnp.bfloat16),
        pltpu.VMEM(held[1:], jnp.float32),
        pltpu.VMEM(held[1:], jnp.bfloat16),
        pltpu.VMEM(held[1:], jnp.bfloat16),
        pltpu.VMEM(tall[1:], jnp.float32),
        pltpu.VMEM((width, grid), jnp.float32),
    ]
    sems = [pairs] * 2 + [around] * 4 + [pairs] * 6
    sems = sems + [(per,), (per, 2), (per,), (per, 2), (per,), (3,)]
    result = pl.pallas_call(
        functools.partial(apply_kernel, first, chans, strips),
        out_shape=[jax.ShapeDtypeStruct(shape, jnp.float32) for shape in outs],
        in_specs=[ANY] * 2,
        out_specs=[ANY] * len(outs),
        scratch_shapes=scratch + [dma(n) for n in sems],
        compiler_params=pltpu.CompilerParams(
            collective_id=0 if first else 1, has_side_effects=True, vmem_limit_bytes=60 * 2**20
        ),
    )(field, radial_op)
    if first:
        return result[5], result[8], result[4], result[3]
    return result[4], result[3]


def couple_kernel(count, last, ints, reals, *refs):
    if last:
        field, direct, mirror, base, out, pots = refs
    else:
        field, direct, mirror, turned, out, flipped, pots = refs
    channels, height, width = field.shape[1:]
    orders = pots.shape[0]
    spacing = 8.0 / count
    row = ints[0] + pl.program_id(0) * height
    row = row + lax.broadcasted_iota(jnp.int32, (height, width), 0)
    col = ints[1] + lax.broadcasted_iota(jnp.int32, (height, width), 1)
    first = row.astype(jnp.float32) * spacing
    second = col.astype(jnp.float32) * spacing
    greater = jnp.maximum(first, second)
    root = jnp.sqrt(greater * greater + 1.0)
    ratio = jnp.minimum(first, second) / root
    pot = 1.0 / root
    for order in range(orders):
        pots[order] = pot
        pot = pot * ratio
    reach = jnp.maximum(row, col)

    def channel(c, carry):
        other = ints[2 + c]
        live = reach < ints[2 + channels + c]
        jobs = [(field, direct, mirror, out)]
        if not last:
            jobs.append((turned, mirror, direct, flipped))
        for tile, straight, crossed, target in jobs:
            real_part = straight[0, c] + crossed[0, other]
            imag_part = straight[1, c] + crossed[1, other]
            for order in range(orders):
                k = ints[2 + 2 * channels + c * orders + order]
                c_real = reals[c * orders + order]
                c_imag = reals[channels * orders + c * orders + order]
                pot = pots[order]
                s_real = pot * tile[0, k]
                s_imag = pot * tile[1, k]
                real_part = real_part + (c_real * s_real - c_imag * s_imag)
                imag_part = imag_part + (c_real * s_imag + c_imag * s_real)
            real_part = jnp.where(live, real_part, 0.0)
            imag_part = jnp.where(live, imag_part, 0.0)
            if last:
                real_part = 2.0 * real_part - base[0, c]
                imag_part = 2.0 * imag_part - base[1, c]
            target[0, c] = real_part
            target[1, c] = imag_part
        return carry

    lax.fori_loop(0, channels, channel, 0)


def couple_tiles(last, count, ints, reals, orders, arrays):
    shape = arrays[0].shape
    height = 16
    block = pl.BlockSpec((2, shape[1], height, shape[3]), lambda n: (0, 0, n, 0))
    smem = pl.BlockSpec(memory_space=pltpu.SMEM)
    return pl.pallas_call(
        functools.partial(couple_kernel, count, last),
        grid=(shape[2] // height,),
        out_shape=[jax.ShapeDtypeStruct(shape, jnp.float32)] * (1 if last else 2),
        in_specs=[smem, smem] + [block] * len(arrays),
        out_specs=[block] * (1 if last else 2),
        scratch_shapes=[pltpu.VMEM((orders, height, shape[3]), jnp.float32)],
    )(ints, reals, *arrays)


def local(wave_field, radial_op, coupling, couple, partner, extent):
    chans = lax.axis_size("chan")
    strips = lax.axis_size("strip")
    per, rows, grid = wave_field.shape[1:]
    width = grid // chans
    orders = coupling.shape[2]
    tiles = (2 * chans, per, rows, width)
    whole = (2, chans * per, rows, width)
    starts = jnp.stack([lax.axis_index("strip") * rows, lax.axis_index("chan") * width])
    ints = jnp.concatenate([starts.astype(jnp.int32), partner, extent, couple.reshape(-1)])
    reals = coupling.reshape(-1)
    flat = wave_field.reshape(2 * per, rows, grid)
    parts = [part.reshape(whole) for part in apply_radial(True, flat, radial_op, tiles)]
    field, turned, direct, mirror = parts
    first_step, first_turned = couple_tiles(
        False, grid, ints, reals, orders, (field, direct, mirror, turned)
    )
    parts = apply_radial(False, first_turned.reshape(tiles), radial_op, tiles)
    parts = [first_step] + [part.reshape(whole) for part in parts] + [field]
    second_step = couple_tiles(True, grid, ints, reals, orders, parts)[0]
    return (first_step, second_step)


def dispatch(wave_field, *rest):
    chans = lax.axis_size("chan")
    strips = lax.axis_size("strip")
    width = wave_field.shape[3] // chans
    if strips == 2 * chans and width % 128 == 0 and wave_field.shape[2] % 16 == 0:
        return local(wave_field, *rest)
    return general(wave_field, *rest)


def solution(mesh):
    placed = (P(None, "chan", "strip", None), P(), P(), P(), P(), P())
    return jax.shard_map(
        dispatch,
        mesh=mesh,
        in_specs=placed,
        out_specs=(P(None, None, "strip", "chan"), P(None, None, "strip", "chan")),
        check_vma=False,
    )
```
